32 devices in a mesh: stream: 4 (over y, core), trans: 8 (over z, x).
Axes of the slice: x: 2, y: 2, z: 4, core: 2. Of those that a mesh axis runs over, the one named last changes fastest.
Arguments:
- populations: float32 [19, 8, 64, 128], P(None, 'stream', 'trans'), may hold values from 0.01 to 0.2
- solid: int32 [8, 64, 128], P('stream', 'trans'), may hold values 0 or 1
- support: int32 [4096], P(('stream', 'trans')), may hold values from 0 to 8062, as said below
- fractions: float32 [3, 4096], P(None, ('stream', 'trans')), may hold values from 0 to 1
- target: float32 [3, 4096], P(None, ('stream', 'trans')), may hold values from -0.1 to 0.1
- area: float32 [4096], P(('stream', 'trans')), may hold values from 1 to 4
Outputs:
- new_populations: float32 [19, 8, 64, 128], P(None, 'stream', 'trans')
- marker_force: float32 [3, 4096], P(None, ('stream', 'trans'))
The draws below stay inside these ranges and needn't reach their ends.
Inputs may be any that keep to these rules, and one draw needn't show every extreme that they name: support[m] = (a * 64 + b) * 128 + e with a = 0 counted inside marker m's streamwise slab m // (128 * 8) (each cube spans the slab's two planes), 0 <= b <= 64 - 2 over the whole first transverse dimension and 0 <= e <= 126.
All inputs are finite; a program needn't handle non-finite values. No bound on the sum of `solid` on one device may be relied on, other than what follows from the above.
Results may differ from the reference program's by a relative error of at most 0.0003.
Values sent between devices are 32-bit elements; how exact they have to be, the bound alone decides.
No kernel may reach another device: no remote copies, remote signals or barrier semaphores. Data moves between devices by JAX's collectives and lax.ppermute only.
A program may use at most 64 MiB of HBM per device.

```python
import math
import jax
import jax.numpy as jnp
from jax import lax

CX = 2
NZ = 128
MK = 128
STEPS = 2
NX = 8
NY = 64
MARKERS = 4096
N_TRANS = 8


def draw_support(key, part):
    subkeys = jax.random.split(key, 6)
    planes = jax.random.randint(subkeys[0], (MARKERS,), 0, CX - 1)
    depths = jax.random.randint(subkeys[1], (MARKERS,), 0, NZ - 1)
    spread_rows = jax.random.randint(subkeys[2], (MARKERS,), 0, NY - 1)
    centres = jax.random.randint(subkeys[3], (4,), 0, NY - 1)
    picker = jax.random.randint(subkeys[4], (MARKERS,), 0, 8)
    jitter = jax.random.randint(subkeys[5], (MARKERS,), -6, 7)
    folded = jnp.clip(centres[picker % 4] + jitter, 0, NY - 2)
    row_values = jnp.where(picker < 4, folded, spread_rows)
    cell_index = (planes * NY + row_values) * NZ + depths
    position = jnp.arange(MARKERS)
    cell_index = jnp.where(position == 0, 0, cell_index)
    cell_index = jnp.where(position == MARKERS - 1, (CX - 2) * NY * NZ + (NY - 2) * NZ + NZ - 2, cell_index)
    return cell_index.astype(jnp.int32)


def with_ends(entries, own_key, least, top_value):
    longest = entries.shape.index(max(entries.shape))
    spots = []
    for shift in (0, 1):
        where = [jax.random.randint(jax.random.fold_in(own_key, axis), (), 0, length) for axis, length in enumerate(entries.shape)]
        where[longest] = (where[longest] + shift) % entries.shape[longest]
        spots.append(tuple(where))
    return entries.at[spots[0]].set(least).at[spots[1]].set(top_value)


def block_scale(stream_key, dims, shards, low, top_value):
    loudness = 1.0
    for axis_at, shards_of in shards:
        draws = jax.random.uniform(jax.random.fold_in(jax.random.fold_in(stream_key, 6), axis_at), (shards_of,), jnp.float32, low / len(shards), top_value / len(shards))
        loudness = loudness * jnp.repeat(jnp.exp(draws), dims[axis_at] // shards_of).reshape((-1,) + (1,) * (len(dims) - 1 - axis_at))
    return loudness


def setup_inputs(seed: int = 0) -> dict:
    key_of = jax.random.split(jax.random.key(seed), 7)
    return {
        "populations": jnp.clip(0.01 + 0.19 * jax.random.uniform(key_of[0], (19, NX, NY, NZ), jnp.float32) ** block_scale(key_of[0], (19, NX, NY, NZ), ((1, 4), (2, 8)), -0.2, 0.2), 0.01, 0.2),
        "solid": with_ends((jax.random.randint(key_of[1], (NX, NY, NZ), 0, 8) < 1).astype(jnp.int32), jax.random.fold_in(key_of[1], 1), 0, 1),
        "support": draw_support(jax.random.fold_in(key_of[6], 71), 0),
        "fractions": jnp.clip(1.0 * jax.random.uniform(key_of[3], (3, MARKERS), jnp.float32) ** block_scale(key_of[3], (3, MARKERS), ((1, 32),), -0.2, 0.2), 0.0, 1.0),
        "target": jnp.clip(jax.random.uniform(key_of[4], (3, MARKERS), jnp.float32, -0.1, 0.1) * block_scale(key_of[4], (3, MARKERS), ((1, 32),), -0.4, 0.0), -0.1, 0.1),
        "area": jnp.clip(jnp.exp(math.log(4.0) - 1.3862944 * jax.random.uniform(key_of[5], (MARKERS,), jnp.float32) ** block_scale(key_of[5], (MARKERS,), ((0, 32),), -0.2, 0.2)), 1.0, 4.0),
    }


velocity_table = ((0, 0, 0), (1, 0, 0), (-1, 0, 0), (0, 1, 0), (0, -1, 0), (0, 0, 1), (0, 0, -1), (1, 1, 0), (-1, -1, 0), (1, -1, 0), (-1, 1, 0), (1, 0, 1), (-1, 0, -1), (1, 0, -1), (-1, 0, 1), (0, 1, 1), (0, -1, -1), (0, 1, -1), (0, -1, 1))
weight_table = (1.0 / 3.0,) + (1.0 / 18.0,) * 6 + (1.0 / 36.0,) * 12
opposite = (0, 2, 1, 4, 3, 6, 5, 8, 7, 10, 9, 12, 11, 14, 13, 16, 15, 18, 17)
relax_base = 0.8
smagorinsky = 0.17

def signed_sum(factors, values):
    running = None
    for factor, value in zip(factors, values):
        if factor != 0:
            signed_term = value if factor > 0 else -value
            running = signed_term if running is None else running + signed_term
    return 0.0 if running is None else running

def moments(fields):
    density = fields[0]
    for member in range(1, 19):
        density = density + fields[member]
    momenta = []
    for dimension in range(3):
        momenta.append(signed_sum([velocity_table[member][dimension] for member in range(19)], [fields[member] for member in range(19)]))
    return (density, momenta)

def collide(fields, density, momenta, forcing, solid):
    velocity = [(momenta[dimension] + 0.5 * forcing[dimension]) / density for dimension in range(3)]
    square = velocity[0] * velocity[0] + velocity[1] * velocity[1] + velocity[2] * velocity[2]
    force_along = velocity[0] * forcing[0] + velocity[1] * forcing[1] + velocity[2] * forcing[2]
    projections = []
    nonequil = []
    for member in range(19):
        projected = signed_sum(velocity_table[member], velocity)
        equilibrium = weight_table[member] * density * (1.0 + 3.0 * projected + 4.5 * projected * projected - 1.5 * square)
        projections.append(projected)
        nonequil.append(fields[member] - equilibrium)
    magnitude_square = 0.0
    for first, second in ((0, 0), (1, 1), (2, 2), (0, 1), (0, 2), (1, 2)):
        component = signed_sum([velocity_table[member][first] * velocity_table[member][second] for member in range(19)], nonequil)
        factor = 1.0 if first == second else 2.0
        magnitude_square = magnitude_square + factor * component * component
    magnitude = jnp.sqrt(magnitude_square)
    relaxation = 0.5 * (relax_base + jnp.sqrt(relax_base * relax_base + 18.0 * math.sqrt(2.0) * smagorinsky * smagorinsky * magnitude / density))
    force_share = 1.0 - 0.5 / relaxation
    outputs = []
    for member in range(19):
        along_force = signed_sum(velocity_table[member], forcing)
        source = force_share * weight_table[member] * (3.0 * (along_force - force_along) + 9.0 * projections[member] * along_force)
        collided = fields[member] - nonequil[member] / relaxation + source
        outputs.append(jnp.where(solid == 1, fields[opposite[member]], collided))
    return jnp.stack(outputs)

def linear_share(fraction, offset):
    return fraction if offset else 1.0 - fraction

def reference(populations, solid, support, fractions, target, area):
    slab_index = jnp.arange(MARKERS, dtype=jnp.int32) // (MK * N_TRANS)
    depth_index = support % NZ
    remainder = support // NZ
    column = remainder % NY
    plane_index = remainder // NY + slab_index * CX
    corners = []
    for shift_x in (0, 1):
        for shift_y in (0, 1):
            for shift_z in (0, 1):
                flat_index = (((plane_index + shift_x) * NY + column + shift_y) * NZ + depth_index + shift_z).astype(jnp.int32)
                weight = linear_share(fractions[0], shift_x) * linear_share(fractions[1], shift_y) * linear_share(fractions[2], shift_z)
                corners.append((flat_index, weight))
    cell_count = NX * NY * NZ
    fields = populations
    force = jnp.zeros((3, MARKERS), jnp.float32)
    for repeat in range(STEPS):
        density, momenta = moments(fields)
        flat_velocity = jnp.stack([momenta[dimension] / density for dimension in range(3)]).reshape(3, cell_count)
        interpolated = jnp.zeros((3, MARKERS), jnp.float32)
        for flat_index, weight in corners:
            interpolated = interpolated + weight * flat_velocity[:, flat_index]
        force = area * (target - interpolated)
        forcing = jnp.zeros((3, cell_count), jnp.float32)
        for flat_index, weight in corners:
            forcing = forcing.at[:, flat_index].add(weight * force)
        forcing = forcing.reshape(3, NX, NY, NZ)
        momentum_stack = jnp.stack(momenta)

        def plane_update(position, fields=fields, density=density, momentum_stack=momentum_stack, forcing=forcing):
            plane_fields = lax.dynamic_index_in_dim(fields, position, 1, keepdims=False)
            plane_density = lax.dynamic_index_in_dim(density, position, 0, keepdims=False)
            plane_momenta = lax.dynamic_index_in_dim(momentum_stack, position, 1, keepdims=False)
            plane_forcing = lax.dynamic_index_in_dim(forcing, position, 1, keepdims=False)
            plane_solid = lax.dynamic_index_in_dim(solid, position, 0, keepdims=False)
            return collide(plane_fields, plane_density, [plane_momenta[0], plane_momenta[1], plane_momenta[2]], plane_forcing, plane_solid)
        collided_all = lax.map(plane_update, jnp.arange(NX, dtype=jnp.int32))
        passed = []
        for member in range(19):
            passed.append(jnp.roll(collided_all[:, member], velocity_table[member], axis=(0, 1, 2)))
        fields = jnp.stack(passed)
    return (fields, force)
```

```python
import math

import jax
import jax.numpy as jnp
from jax import lax
from jax.experimental import pallas as pl
from jax.experimental.pallas import tpu as pltpu
from jax.sharding import PartitionSpec as P

STEPS = 2
HALO = 4

velocity_table = (
    (0, 0, 0),
    (1, 0, 0),
    (-1, 0, 0),
    (0, 1, 0),
    (0, -1, 0),
    (0, 0, 1),
    (0, 0, -1),
    (1, 1, 0),
    (-1, -1, 0),
    (1, -1, 0),
    (-1, 1, 0),
    (1, 0, 1),
    (-1, 0, -1),
    (1, 0, -1),
    (-1, 0, 1),
    (0, 1, 1),
    (0, -1, -1),
    (0, 1, -1),
    (0, -1, 1),
)
weight_table = (1.0 / 3.0,) + (1.0 / 18.0,) * 6 + (1.0 / 36.0,) * 12
relax_base = 0.8
smagorinsky = 0.17
forward_x = tuple(i for i in range(19) if velocity_table[i][0] == 1)
backward_x = tuple(i for i in range(19) if velocity_table[i][0] == -1)
pairs = tuple((i, i + 1) for i in range(1, 19, 2))


def signed_sum(factors, values):
    running = None
    for factor, value in zip(factors, values):
        if factor != 0:
            if running is None:
                running = value if factor > 0 else -value
            else:
                running = running + value if factor > 0 else running - value
    return running


def tree_sum(values):
    values = list(values)
    while len(values) > 1:
        values = [
            values[k] + values[k + 1] if k + 1 < len(values) else values[k]
            for k in range(0, len(values), 2)
        ]
    return values[0]


def moments(f):
    plus = {i: f[i] + f[j] for i, j in pairs}
    minus = {i: f[i] - f[j] for i, j in pairs}
    density = tree_sum([f[0]] + [plus[i] for i, _ in pairs])
    momenta = []
    for d in range(3):
        momenta.append(
            signed_sum(
                [velocity_table[i][d] for i, _ in pairs], [minus[i] for i, _ in pairs]
            )
        )
    second = {}
    for a, b in ((0, 0), (1, 1), (2, 2), (0, 1), (0, 2), (1, 2)):
        second[(a, b)] = signed_sum(
            [velocity_table[i][a] * velocity_table[i][b] for i, _ in pairs],
            [plus[i] for i, _ in pairs],
        )
    return density, momenta, second


def collide(f, density, momenta, second, force, solid):
    inverse = 1.0 / density
    u = [(momenta[d] + 0.5 * force[d]) * inverse for d in range(3)]
    square = u[0] * u[0] + u[1] * u[1] + u[2] * u[2]
    along = u[0] * force[0] + u[1] * force[1] + u[2] * force[2]
    magnitude = None
    third = density * (1.0 / 3.0)
    for a, b in ((0, 0), (1, 1), (2, 2), (0, 1), (0, 2), (1, 2)):
        part = second[(a, b)] - density * (u[a] * u[b])
        if a == b:
            part = part - third
            term = part * part
        else:
            term = 2.0 * part * part
        magnitude = term if magnitude is None else magnitude + term
    magnitude = jnp.sqrt(magnitude)
    tau = 0.5 * (
        relax_base
        + jnp.sqrt(
            relax_base * relax_base
            + (18.0 * math.sqrt(2.0) * smagorinsky * smagorinsky) * magnitude * inverse
        )
    )
    omega = 1.0 / tau
    keep = 1.0 - omega
    share = 1.0 - 0.5 * omega
    scaled = omega * density
    q = [scaled * u[d] + share * force[d] for d in range(3)]
    base = scaled * (1.0 - 1.5 * square) - 3.0 * share * along
    out = [None] * 19
    out[0] = jnp.where(solid, f[0], keep * f[0] + weight_table[0] * base)
    for i, j in pairs:
        c = velocity_table[i]
        p = signed_sum(c, u)
        cq = signed_sum(c, q)
        w = weight_table[i]
        even = w * (base + 9.0 * p * (cq - 0.5 * scaled * p))
        odd = (3.0 * w) * cq
        out[i] = jnp.where(solid, f[j], keep * f[i] + (even + odd))
        out[j] = jnp.where(solid, f[i], keep * f[j] + (even - odd))
    return out


def split_pieces(value):
    high = value.astype(jnp.bfloat16)
    low = (value - high.astype(jnp.float32)).astype(jnp.bfloat16)
    return high, low


def marker_pass(velocity, marker_ref, row_start, row_count, total_rows, depth_count):
    planes, rows, depth = velocity[0].shape
    cells = planes * rows
    blocks = marker_ref.shape[0]
    width = marker_ref.shape[2]
    stacked = jnp.concatenate([v.reshape(cells, depth) for v in velocity], axis=0)
    shifted = pltpu.roll(stacked, depth - 1, 1)
    high, low = split_pieces(stacked)
    high_next, low_next = split_pieces(shifted)
    left = jnp.concatenate(
        [
            jnp.concatenate([high, low], axis=1),
            jnp.concatenate([high_next, low_next], axis=1),
        ],
        axis=0,
    )
    group = 2 if blocks % 2 == 0 else 1
    lanes = group * width
    row_iota = lax.broadcasted_iota(jnp.int32, (rows, lanes), 0)
    relative = jnp.where(row_iota < rows - HALO, row_iota, row_iota - rows)
    row_id = relative + row_start
    row_id = jnp.where(row_id < 0, row_id + total_rows, row_id)
    row_id = jnp.where(row_id >= total_rows, row_id - total_rows, row_id)
    depth_iota = lax.broadcasted_iota(jnp.int32, (depth, lanes), 0)
    total = None
    owned = []
    for start in range(0, blocks, group):
        parts = [marker_ref[start + k] for k in range(group)]
        data = parts[0] if group == 1 else jnp.concatenate(parts, axis=1)
        cell = data[0:1].astype(jnp.int32)
        column = cell // depth_count
        place = cell - column * depth_count
        fx, fy, fz = data[1:2], data[2:3], data[3:4]
        area = data[7:8]
        selector = jnp.where(depth_iota == place, 1.0, 0.0).astype(jnp.bfloat16)
        both = jnp.concatenate([selector, selector], axis=0)
        gathered = lax.dot_general(
            left, both, (((1,), (0,)), ((), ())), preferred_element_type=jnp.float32
        )
        row_weight = jnp.where(row_id == column, 1.0 - fy, 0.0) + jnp.where(
            row_id == column + 1, fy, 0.0
        )
        pair_weight = jnp.concatenate([row_weight * (1.0 - fx), row_weight * fx], axis=0)
        near = pair_weight * (1.0 - fz)
        far = pair_weight * fz
        offset = column - row_start
        own = jnp.logical_and(offset >= 0, offset < row_count)
        force = []
        for c in range(3):
            terms = near * gathered[c * cells : (c + 1) * cells] + far * gathered[
                (3 + c) * cells : (4 + c) * cells
            ]
            value = jnp.sum(terms, axis=0, keepdims=True)
            force.append(area * (data[4 + c : 5 + c] - value))
        owned.append([jnp.where(own, value, 0.0) for value in force])
        spread = jnp.concatenate(
            [near * value for value in force] + [far * value for value in force], axis=0
        )
        spread_high, spread_low = split_pieces(spread)
        added = lax.dot_general(
            jnp.concatenate([spread_high, spread_low], axis=0),
            selector,
            (((1,), (1,)), ((), ())),
            preferred_element_type=jnp.float32,
        )
        total = added if total is None else total + added
    near_part = total[0 : 3 * cells] + total[6 * cells : 9 * cells]
    far_part = total[3 * cells : 6 * cells] + total[9 * cells : 12 * cells]
    grid = near_part + pltpu.roll(far_part, 1, 1)
    forcing = [
        grid[c * cells : (c + 1) * cells].reshape(planes, rows, depth) for c in range(3)
    ]
    return forcing, owned, group, width


def moved(value, member):
    _, step_y, step_z = velocity_table[member]
    if step_y:
        value = pltpu.roll(value, step_y % value.shape[1], 1)
    if step_z:
        value = pltpu.roll(value, step_z % value.shape[2], 2)
    return value


def first_kernel(own_ref, after_ref, before_ref, solid_ref, marker_ref, start_ref,
                 next_ref, up_ref, down_ref, solid_out_ref, window,
                 *, total_rows, depth_count):
    row_count = own_ref.shape[2]
    window[0:19, :, 0:row_count, :] = own_ref[...]
    window[19, :, 0:row_count, :] = solid_ref[...].astype(jnp.float32)
    window[:, :, row_count : row_count + HALO, :] = after_ref[...]
    window[:, :, row_count + HALO :, :] = before_ref[...]
    f = [window[i] for i in range(19)]
    solid_values = window[19]
    solid_out_ref[...] = solid_values
    density, momenta, second = moments(f)
    inverse = 1.0 / density
    velocity = [m * inverse for m in momenta]
    row_start = start_ref[0]
    forcing, _, _, _ = marker_pass(
        velocity, marker_ref, row_start, row_count, total_rows, depth_count
    )
    out = collide(f, density, momenta, second, forcing, solid_values == 1.0)
    for i in range(19):
        value = moved(out[i], i)
        step_x = velocity_table[i][0]
        if step_x == 0:
            next_ref[i] = value
        elif step_x == 1:
            next_ref[i, 1] = value[0]
            up_ref[forward_x.index(i)] = value[1]
        else:
            next_ref[i, 0] = value[1]
            down_ref[backward_x.index(i)] = value[0]


def last_kernel(next_ref, low_ref, high_ref, solid_ref, marker_ref, start_ref,
                out_ref, up_ref, down_ref, force_ref,
                *, row_count, total_rows, depth_count):
    f = []
    for i in range(19):
        step_x = velocity_table[i][0]
        if step_x == 0:
            f.append(next_ref[i])
        elif step_x == 1:
            f.append(jnp.stack([low_ref[forward_x.index(i)], next_ref[i, 1]]))
        else:
            f.append(jnp.stack([next_ref[i, 0], high_ref[backward_x.index(i)]]))
    density, momenta, second = moments(f)
    inverse = 1.0 / density
    velocity = [m * inverse for m in momenta]
    row_start = start_ref[0]
    forcing, owned, group, width = marker_pass(
        velocity, marker_ref, row_start, row_count, total_rows, depth_count
    )
    for position, values in enumerate(owned):
        for k in range(group):
            for c in range(3):
                force_ref[position * group + k, c : c + 1, :] = values[c][
                    :, k * width : (k + 1) * width
                ]
    out = collide(f, density, momenta, second, forcing, solid_ref[...] == 1.0)
    for i in range(19):
        value = moved(out[i], i)[:, 0:row_count]
        step_x = velocity_table[i][0]
        if step_x == 0:
            out_ref[i] = value
        elif step_x == 1:
            out_ref[i, 1] = value[0]
            up_ref[forward_x.index(i)] = value[1]
        else:
            out_ref[i, 0] = value[1]
            down_ref[backward_x.index(i)] = value[0]


def ring(count, step):
    return [(i, (i + step) % count) for i in range(count)]


def exchanged(low_bound, high_bound, axis):
    count = lax.axis_size(axis)
    from_low = lax.ppermute(high_bound, axis, ring(count, 1))
    from_high = lax.ppermute(low_bound, axis, ring(count, -1))
    return from_low, from_high


def per_device(populations, solid, support, fractions, target, area):
    plane_count, row_count, depth_count = populations.shape[1:]
    own_markers = support.shape[0]
    groups = lax.axis_size("trans")
    total_rows = row_count * groups
    rows = row_count + 2 * HALO
    row_start = (lax.axis_index("trans") * row_count).astype(jnp.int32).reshape(1)

    packed = jnp.concatenate(
        [support.astype(jnp.float32)[None], fractions, target, area[None]], axis=0
    )
    rim = jnp.concatenate([populations, solid.astype(jnp.float32)[None]], axis=0)
    before, after = exchanged(
        rim[:, :, :HALO], rim[:, :, row_count - HALO :], "trans"
    )
    copies = jnp.broadcast_to(packed[None], (groups,) + packed.shape)
    markers = lax.all_to_all(copies, "trans", 0, 0, tiled=False)

    vmem = pl.BlockSpec(memory_space=pltpu.VMEM)
    smem = pl.BlockSpec(memory_space=pltpu.SMEM)
    f32 = jnp.float32
    side = len(forward_x)

    def first(*refs):
        first_kernel(*refs, total_rows=total_rows, depth_count=depth_count)

    following, up, down, solid_window = pl.pallas_call(
        first,
        out_shape=(
            jax.ShapeDtypeStruct((19, plane_count, rows, depth_count), f32),
            jax.ShapeDtypeStruct((side, rows, depth_count), f32),
            jax.ShapeDtypeStruct((side, rows, depth_count), f32),
            jax.ShapeDtypeStruct((plane_count, rows, depth_count), f32),
        ),
        in_specs=[vmem, vmem, vmem, vmem, vmem, smem],
        out_specs=(vmem, vmem, vmem, vmem),
        scratch_shapes=[pltpu.VMEM((20, plane_count, rows, depth_count), f32)],
        name="first_step",
    )(populations, after, before, solid, markers, row_start)
    from_low, from_high = exchanged(down, up, "stream")

    def last(*refs):
        last_kernel(*refs, row_count=row_count, total_rows=total_rows, depth_count=depth_count)

    outgoing, up, down, force = pl.pallas_call(
        last,
        out_shape=(
            jax.ShapeDtypeStruct((19, plane_count, row_count, depth_count), f32),
            jax.ShapeDtypeStruct((side, row_count, depth_count), f32),
            jax.ShapeDtypeStruct((side, row_count, depth_count), f32),
            jax.ShapeDtypeStruct((groups, 3, own_markers), f32),
        ),
        in_specs=[vmem, vmem, vmem, vmem, vmem, smem],
        out_specs=(vmem, vmem, vmem, vmem),
        name="last_step",
    )(following, from_low, from_high, solid_window, markers, row_start)
    from_low, from_high = exchanged(down, up, "stream")
    own_force = jnp.sum(lax.all_to_all(force, "trans", 0, 0, tiled=False), axis=0)
    planes = []
    for i in range(19):
        step_x = velocity_table[i][0]
        if step_x == 0:
            planes.append(outgoing[i])
        elif step_x == 1:
            planes.append(jnp.stack([from_low[forward_x.index(i)], outgoing[i, 1]]))
        else:
            planes.append(jnp.stack([outgoing[i, 0], from_high[backward_x.index(i)]]))
    return (jnp.stack(planes), own_force)


def solution(mesh):
    placed = (
        P(None, "stream", "trans", None),
        P("stream", "trans", None),
        P(("stream", "trans")),
        P(None, ("stream", "trans")),
        P(None, ("stream", "trans")),
        P(("stream", "trans")),
    )
    return jax.shard_map(
        per_device,
        mesh=mesh,
        in_specs=placed,
        out_specs=(P(None, "stream", "trans", None), P(None, ("stream", "trans"))),
        check_vma=False,
    )
```

```python
import math

import jax
import jax.numpy as jnp
from jax import lax
from jax.experimental import pallas as pl
from jax.experimental.pallas import tpu as pltpu
from jax.sharding import PartitionSpec as P


HALO = 4

velocity_table = (
    (0, 0, 0),
    (1, 0, 0),
    (-1, 0, 0),
    (0, 1, 0),
    (0, -1, 0),
    (0, 0, 1),
    (0, 0, -1),
    (1, 1, 0),
    (-1, -1, 0),
    (1, -1, 0),
    (-1, 1, 0),
    (1, 0, 1),
    (-1, 0, -1),
    (1, 0, -1),
    (-1, 0, 1),
    (0, 1, 1),
    (0, -1, -1),
    (0, 1, -1),
    (0, -1, 1),
)
weight_table = (1.0 / 3.0,) + (1.0 / 18.0,) * 6 + (1.0 / 36.0,) * 12
relax_base = 0.8
smagorinsky = 0.17
forward_x = tuple(i for i in range(19) if velocity_table[i][0] == 1)
backward_x = tuple(i for i in range(19) if velocity_table[i][0] == -1)
pairs = tuple((i, i + 1) for i in range(1, 19, 2))


def signed_sum(factors, values):
    running = None
    for factor, value in zip(factors, values):
        if factor != 0:
            if running is None:
                running = value if factor > 0 else -value
            else:
                running = running + value if factor > 0 else running - value
    return running


def tree_sum(values):
    values = list(values)
    while len(values) > 1:
        values = [
            values[k] + values[k + 1] if k + 1 < len(values) else values[k]
            for k in range(0, len(values), 2)
        ]
    return values[0]


def moments(f):
    plus = {i: f[i] + f[j] for i, j in pairs}
    minus = {i: f[i] - f[j] for i, j in pairs}
    density = tree_sum([f[0]] + [plus[i] for i, _ in pairs])
    momenta = []
    for d in range(3):
        momenta.append(
            signed_sum(
                [velocity_table[i][d] for i, _ in pairs], [minus[i] for i, _ in pairs]
            )
        )
    second = {}
    for a, b in ((0, 0), (1, 1), (2, 2), (0, 1), (0, 2), (1, 2)):
        second[(a, b)] = signed_sum(
            [velocity_table[i][a] * velocity_table[i][b] for i, _ in pairs],
            [plus[i] for i, _ in pairs],
        )
    return density, momenta, second


def collide(f, density, momenta, second, force, solid):
    inverse = 1.0 / density
    u = [(momenta[d] + 0.5 * force[d]) * inverse for d in range(3)]
    square = u[0] * u[0] + u[1] * u[1] + u[2] * u[2]
    along = u[0] * force[0] + u[1] * force[1] + u[2] * force[2]
    magnitude = None
    third = density * (1.0 / 3.0)
    for a, b in ((0, 0), (1, 1), (2, 2), (0, 1), (0, 2), (1, 2)):
        part = second[(a, b)] - density * (u[a] * u[b])
        if a == b:
            part = part - third
            term = part * part
        else:
            term = 2.0 * part * part
        magnitude = term if magnitude is None else magnitude + term
    magnitude = jnp.sqrt(magnitude)
    tau = 0.5 * (
        relax_base
        + jnp.sqrt(
            relax_base * relax_base
            + (18.0 * math.sqrt(2.0) * smagorinsky * smagorinsky) * magnitude * inverse
        )
    )
    omega = 1.0 / tau
    keep = 1.0 - omega
    share = 1.0 - 0.5 * omega
    scaled = omega * density
    q = [scaled * u[d] + share * force[d] for d in range(3)]
    base = scaled * (1.0 - 1.5 * square) - 3.0 * share * along
    out = [None] * 19
    out[0] = jnp.where(solid, f[0], keep * f[0] + weight_table[0] * base)
    for i, j in pairs:
        c = velocity_table[i]
        p = signed_sum(c, u)
        cq = signed_sum(c, q)
        w = weight_table[i]
        even = w * (base + 9.0 * p * (cq - 0.5 * scaled * p))
        odd = (3.0 * w) * cq
        out[i] = jnp.where(solid, f[j], keep * f[i] + (even + odd))
        out[j] = jnp.where(solid, f[i], keep * f[j] + (even - odd))
    return out


def split_pieces(value):
    high = value.astype(jnp.bfloat16)
    low = (value - high.astype(jnp.float32)).astype(jnp.bfloat16)
    return high, low


class Markers:
    def __init__(self, marker_ref, row_start, rows, total_rows, depth):
        self.ref = marker_ref
        self.blocks = marker_ref.shape[0]
        self.width = marker_ref.shape[2]
        self.group = 2 if self.blocks % 2 == 0 else 1
        self.depth = depth
        lanes = self.group * self.width
        row_iota = lax.broadcasted_iota(jnp.int32, (rows, lanes), 0)
        relative = jnp.where(row_iota < rows - HALO, row_iota, row_iota - rows)
        row_id = relative + row_start
        row_id = jnp.where(row_id < 0, row_id + total_rows, row_id)
        self.row_id = jnp.where(row_id >= total_rows, row_id - total_rows, row_id)
        self.depth_iota = lax.broadcasted_iota(jnp.int32, (depth, lanes), 0)

    def starts(self):
        return range(0, self.blocks, self.group)

    def weights(self, start):
        parts = [self.ref[start + k] for k in range(self.group)]
        data = parts[0] if self.group == 1 else jnp.concatenate(parts, axis=1)
        cell = data[0:1].astype(jnp.int32)
        column = cell // self.depth
        place = cell - column * self.depth
        fx, fy, fz = data[1:2], data[2:3], data[3:4]
        selector = jnp.where(self.depth_iota == place, 1.0, 0.0).astype(jnp.bfloat16)
        row_weight = jnp.where(self.row_id == column, 1.0 - fy, 0.0) + jnp.where(
            self.row_id == column + 1, fy, 0.0
        )
        pair_weight = jnp.concatenate([row_weight * (1.0 - fx), row_weight * fx], axis=0)
        return data, column, selector, pair_weight * (1.0 - fz), pair_weight * fz


def velocity_operand(velocity):
    planes, rows, depth = velocity[0].shape
    stacked = jnp.concatenate([v.reshape(planes * rows, depth) for v in velocity], axis=0)
    shifted = pltpu.roll(stacked, depth - 1, 1)
    return jnp.concatenate(
        [
            jnp.concatenate(split_pieces(stacked), axis=1),
            jnp.concatenate(split_pieces(shifted), axis=1),
        ],
        axis=0,
    )


def marker_force(left, data, selector, near, far):
    cells = near.shape[0]
    gathered = lax.dot_general(
        left,
        jnp.concatenate([selector, selector], axis=0),
        (((1,), (0,)), ((), ())),
        preferred_element_type=jnp.float32,
    )
    force = []
    for c in range(3):
        terms = near * gathered[c * cells : (c + 1) * cells] + far * gathered[
            (3 + c) * cells : (4 + c) * cells
        ]
        value = jnp.sum(terms, axis=0, keepdims=True)
        force.append(data[7:8] * (data[4 + c : 5 + c] - value))
    return force


def spread_force(force, selector, near, far):
    spread = jnp.concatenate(
        [near * value for value in force] + [far * value for value in force], axis=0
    )
    return lax.dot_general(
        jnp.concatenate(split_pieces(spread), axis=0),
        selector,
        (((1,), (1,)), ((), ())),
        preferred_element_type=jnp.float32,
    )


def forcing_fields(total, planes, rows, depth):
    cells = planes * rows
    near = total[0 : 3 * cells] + total[6 * cells : 9 * cells]
    far = total[3 * cells : 6 * cells] + total[9 * cells : 12 * cells]
    grid = near + pltpu.roll(far, 1, 1)
    return [grid[c * cells : (c + 1) * cells].reshape(planes, rows, depth) for c in range(3)]


def moved(value, member):
    _, step_y, step_z = velocity_table[member]
    if step_y:
        value = pltpu.roll(value, step_y % value.shape[1], 1)
    if step_z:
        value = pltpu.roll(value, step_z % value.shape[2], 2)
    return value


def place_bits(place_ref):
    place = place_ref[0]
    return place >> 2, ((place >> 1) & 1) == 0, (place & 1) == 0


def pack_kernel(populations_hbm, solid_hbm, support_hbm, fractions_hbm, target_hbm, area_hbm,
                place_ref, packed_ref, own_ref, near_ref, far_ref,
                solid_buf, support_buf, fractions_buf, target_buf, area_buf, sems):
    small = [
        pltpu.make_async_copy(source, target, sems.at[k])
        for k, (source, target) in enumerate(
            (
                (support_hbm, support_buf),
                (fractions_hbm, fractions_buf),
                (target_hbm, target_buf),
                (area_hbm, area_buf),
            )
        )
    ]
    large = [
        pltpu.make_async_copy(solid_hbm, solid_buf, sems.at[4]),
        pltpu.make_async_copy(populations_hbm, own_ref.at[0:19], sems.at[5]),
    ]
    for copy in small + large:
        copy.start()
    for copy in small:
        copy.wait()
    packed_ref[0:1, :] = support_buf[...].astype(jnp.float32)
    packed_ref[1:4, :] = fractions_buf[...]
    packed_ref[4:7, :] = target_buf[...]
    packed_ref[7:8, :] = area_buf[...]
    for copy in large:
        copy.wait()
    own_ref[19] = solid_buf[...].astype(jnp.float32)
    _, even, _ = place_bits(place_ref)
    rows = own_ref.shape[2]
    for i in range(20):
        low = own_ref[i, :, 0:HALO, :]
        high = own_ref[i, :, rows - HALO :, :]
        near_ref[i] = jnp.where(even, high, low)
        far_ref[i] = jnp.where(even, low, high)


def store_moved(out, next_ref, near_ref, far_ref, even, rows):
    for k, (i, j) in enumerate(zip(forward_x, backward_x)):
        up = moved(out[i], i)[:, 0:rows]
        down = moved(out[j], j)[:, 0:rows]
        next_ref[i, 1] = up[0]
        next_ref[j, 0] = down[1]
        near_ref[k] = jnp.where(even, up[1], down[0])
        far_ref[k] = jnp.where(even, down[0], up[1])
    for i in range(19):
        if velocity_table[i][0] == 0:
            next_ref[i] = moved(out[i], i)[:, 0:rows]


def joined(next_ref, near_ref, far_ref, even):
    f = [None] * 19
    for k, (i, j) in enumerate(zip(forward_x, backward_x)):
        near, far = near_ref[k], far_ref[k]
        f[i] = jnp.stack([jnp.where(even, far, near), next_ref[i, 1]])
        f[j] = jnp.stack([next_ref[j, 0], jnp.where(even, near, far)])
    for i in range(19):
        if velocity_table[i][0] == 0:
            f[i] = next_ref[i]
    return f


def first_kernel(own_ref, rim_near_ref, rim_far_ref, marker_ref, place_ref,
                 next_ref, near_ref, far_ref, solid_out_ref, window, *, total_rows):
    row_count = own_ref.shape[2]
    _, planes, rows, depth = window.shape
    row_start, even, stream_even = place_bits(place_ref)
    window[:, :, 0:row_count, :] = own_ref[...]
    for i in range(20):
        near, far = rim_near_ref[i], rim_far_ref[i]
        window[i, :, row_count : row_count + HALO, :] = jnp.where(even, near, far)
        window[i, :, row_count + HALO :, :] = jnp.where(even, far, near)
    f = [window[i] for i in range(19)]
    solid_values = window[19]
    solid_out_ref[...] = solid_values
    density, momenta, second = moments(f)
    inverse = 1.0 / density
    left = velocity_operand([m * inverse for m in momenta])
    markers = Markers(marker_ref, row_start, rows, total_rows, depth)
    total = None
    for start in markers.starts():
        data, _, selector, near, far = markers.weights(start)
        force = marker_force(left, data, selector, near, far)
        added = spread_force(force, selector, near, far)
        total = added if total is None else total + added
    forcing = forcing_fields(total, planes, rows, depth)
    out = collide(f, density, momenta, second, forcing, solid_values == 1.0)
    store_moved(out, next_ref, near_ref, far_ref, stream_even, rows)


def force_kernel(next_ref, near_ref, far_ref, marker_ref, place_ref, force_ref, owned_ref,
                 *, row_count, total_rows):
    row_start, _, stream_even = place_bits(place_ref)
    f = joined(next_ref, near_ref, far_ref, stream_even)
    _, rows, depth = f[0].shape
    density, momenta, _ = moments(f)
    inverse = 1.0 / density
    left = velocity_operand([m * inverse for m in momenta])
    markers = Markers(marker_ref, row_start, rows, total_rows, depth)
    width = markers.width
    for start in markers.starts():
        data, column, selector, near, far = markers.weights(start)
        force = marker_force(left, data, selector, near, far)
        offset = column - row_start
        own = jnp.logical_and(offset >= 0, offset < row_count)
        for c in range(3):
            kept = jnp.where(own, force[c], 0.0)
            for k in range(markers.group):
                span = slice(k * width, (k + 1) * width)
                force_ref[start + k, c : c + 1, :] = force[c][:, span]
                owned_ref[start + k, c : c + 1, :] = kept[:, span]


def last_kernel(next_ref, near_in_ref, far_in_ref, solid_ref, marker_ref, force_ref, place_ref,
                out_ref, near_ref, far_ref, *, row_count, total_rows):
    row_start, _, stream_even = place_bits(place_ref)
    f = joined(next_ref, near_in_ref, far_in_ref, stream_even)
    planes, rows, depth = f[0].shape
    density, momenta, second = moments(f)
    markers = Markers(marker_ref, row_start, rows, total_rows, depth)
    total = None
    for start in markers.starts():
        _, _, selector, near, far = markers.weights(start)
        blocks = [force_ref[start + k] for k in range(markers.group)]
        values = blocks[0] if markers.group == 1 else jnp.concatenate(blocks, axis=1)
        added = spread_force([values[c : c + 1] for c in range(3)], selector, near, far)
        total = added if total is None else total + added
    forcing = forcing_fields(total, planes, rows, depth)
    out = collide(f, density, momenta, second, forcing, solid_ref[...] == 1.0)
    store_moved(out, out_ref, near_ref, far_ref, stream_even, row_count)


def join_kernel(next_ref, near_ref, far_ref, place_ref, out_ref):
    _, _, stream_even = place_bits(place_ref)
    for i, value in enumerate(joined(next_ref, near_ref, far_ref, stream_even)):
        out_ref[i] = value


def crossed(count, mask):
    return [(i, i ^ mask) for i in range(count)]


def paired(count, shift):
    swap = []
    for i in range(shift, count, 2):
        a, b = i % count, (i + 1) % count
        swap += [(a, b), (b, a)]
    return swap


def swapped(near, far, axis):
    count = lax.axis_size(axis)
    far = lax.ppermute(far, axis, paired(count, 1))
    near = lax.ppermute(near, axis, paired(count, 0))
    return near, far


def local(array):
    return pltpu.with_memory_space_constraint(array, pltpu.VMEM)


def call(kernel, inputs, outputs, place, scratch=(), in_hbm=False, out_hbm=False, **sizes):
    vmem = pl.BlockSpec(memory_space=pltpu.VMEM)
    smem = pl.BlockSpec(memory_space=pltpu.SMEM)
    anywhere = pl.BlockSpec(memory_space=pl.ANY)

    def body(*refs):
        kernel(*refs, **sizes)

    def result(shape):
        if out_hbm:
            return jax.ShapeDtypeStruct(shape, jnp.float32)
        return pltpu.VMEM(shape, jnp.float32)

    return pl.pallas_call(
        body,
        out_shape=tuple(result(s) for s in outputs),
        in_specs=[anywhere if in_hbm else vmem] * len(inputs) + [smem],
        out_specs=tuple(vmem for _ in outputs),
        scratch_shapes=list(scratch),
    )(*[a if in_hbm else local(a) for a in inputs], place)


def per_device(populations, solid, support, fractions, target, area):
    plane_count, row_count, depth_count = populations.shape[1:]
    own_markers = support.shape[0]
    groups = lax.axis_size("trans")
    total_rows = row_count * groups
    rows = row_count + 2 * HALO
    rank = lax.axis_index("trans")
    slab = lax.axis_index("stream")
    place = (rank * (4 * row_count) + (rank % 2) * 2 + slab % 2).astype(jnp.int32).reshape(1)
    side = len(forward_x)
    rim_shape = (20, plane_count, HALO, depth_count)
    f32 = jnp.float32

    packed, own, near, far = call(
        pack_kernel,
        [populations, solid, support[None], fractions, target, area[None]],
        [(8, own_markers), (20, plane_count, row_count, depth_count), rim_shape, rim_shape],
        place,
        scratch=[
            pltpu.VMEM(solid.shape, jnp.int32),
            pltpu.VMEM((1, own_markers), jnp.int32),
            pltpu.VMEM((3, own_markers), f32),
            pltpu.VMEM((3, own_markers), f32),
            pltpu.VMEM((1, own_markers), f32),
            pltpu.SemaphoreType.DMA((6,)),
        ],
        in_hbm=True,
    )
    near, far = swapped(near, far, "trans")
    markers = packed[None]
    mask = 1
    while mask < groups:
        arrived = lax.ppermute(markers, "trans", crossed(groups, mask))
        markers = jnp.concatenate([markers, arrived], axis=0)
        mask *= 2
    window_shape = (19, plane_count, rows, depth_count)
    side_shape = (side, rows, depth_count)
    following, near, far, solid_window = call(
        first_kernel,
        [own, near, far, markers],
        [window_shape, side_shape, side_shape, (plane_count, rows, depth_count)],
        place,
        scratch=[pltpu.VMEM((20, plane_count, rows, depth_count), f32)],
        total_rows=total_rows,
    )
    near, far = swapped(near, far, "stream")
    force, owned = call(
        force_kernel,
        [following, near, far, markers],
        [(groups, 3, own_markers)] * 2,
        place,
        row_count=row_count,
        total_rows=total_rows,
    )
    mask = groups // 2
    while mask:
        arrived = lax.ppermute(owned[mask : 2 * mask], "trans", crossed(groups, mask))
        owned = owned[:mask] + arrived
        mask //= 2
    own_force = owned[0]
    outgoing, near, far = call(
        last_kernel,
        [following, near, far, solid_window, markers, force],
        [(19, plane_count, row_count, depth_count)] + [(side, row_count, depth_count)] * 2,
        place,
        row_count=row_count,
        total_rows=total_rows,
    )
    near, far = swapped(near, far, "stream")
    (result,) = call(
        join_kernel,
        [outgoing, near, far],
        [(19, plane_count, row_count, depth_count)],
        place,
        out_hbm=True,
    )
    return (result, own_force)


def solution(mesh):
    placed = (
        P(None, "stream", "trans", None),
        P("stream", "trans", None),
        P(("stream", "trans")),
        P(None, ("stream", "trans")),
        P(None, ("stream", "trans")),
        P(("stream", "trans")),
    )

    return jax.shard_map(
        per_device,
        mesh=mesh,
        in_specs=placed,
        out_specs=(P(None, "stream", "trans", None), P(None, ("stream", "trans"))),
        check_vma=False,
    )
```
